32 devices in a mesh: seq: 4 (over y, x), outer: 8 (over z, core).
Axes of the slice: x: 2, y: 2, z: 4, core: 2. Of those that a mesh axis runs over, the one named last changes fastest.
Arguments:
- queries: bfloat16 [16384, 2048], P(('outer', 'seq')), may hold values from -41 to 41
- keys: bfloat16 [16384, 512], P(('outer', 'seq')), may hold values from -6 to 6
- values: bfloat16 [16384, 512], P(('outer', 'seq')), may hold values from -6 to 6
Outputs:
- attended: bfloat16 [16384, 2048], P(('outer', 'seq'))
The draws below stay inside these ranges and needn't reach their ends.
All inputs are finite; a program needn't handle non-finite values.
Results may differ from the reference program's by a relative error of at most 0.014.
Values may be sent and summed in bfloat16 or wider, within the bound.
A program may use at most 64 MiB of HBM per device.

```python
import jax
import jax.numpy as jnp
from jax import lax

HD = 128
QHEADS = 16
KVHEADS = 4
BLOCK = 128
POOL = 8
TOKENS = 16384


def draw_shared_keys(key):
    source = jax.random.fold_in(key, 101)
    return jax.random.truncated_normal(source, -6.0, 6.0, (TOKENS, KVHEADS * HD), jnp.float32)


def draw_keys(key, part):
    return draw_shared_keys(key).astype(jnp.bfloat16)


def draw_queries(key, part):
    drawn_draw = jax.random.truncated_normal(jax.random.fold_in(key, 202), -6.0, 6.0, (TOKENS, QHEADS * HD), jnp.float32)
    return drawn_draw.astype(jnp.bfloat16)


def level_of(key, dims, cuts, least, largest):
    def one(dim, blocks):
        heights = jax.random.uniform(jax.random.fold_in(jax.random.fold_in(key, 6), dim), (blocks,), jnp.float32, least / len(cuts), largest / len(cuts))
        return jnp.repeat(jnp.exp(heights), dims[dim] // blocks).reshape((-1,) + (1,) * (len(dims) - dim - 1))

    factor_of = one(*cuts[0])
    for cut in cuts[1:]:
        factor_of = factor_of * one(*cut)
    return factor_of


def centred(key, shape, width, limit, shards=(), kind=jnp.bfloat16):
    values = jax.random.normal(key, shape, jnp.float32) * width
    if len(shards) > 0:
        values = level_of(key, shape, shards, -0.22, 0.18) * values
    return jnp.clip(values, min=-limit, max=limit).astype(kind)


def setup_inputs(seed: int = 0) -> dict:
    arg_keys = jax.random.split(jax.random.key(seed), 4)
    queries = draw_queries(jax.random.fold_in(arg_keys[3], 71), 0)
    keys = draw_keys(jax.random.fold_in(arg_keys[3], 71), 0)
    values = centred(arg_keys[2], (TOKENS, KVHEADS * HD), 1.0, 6.0, ((0, 32),))
    return dict(queries=queries, keys=keys, values=values)


def pool_level(element_item):
    span_length = element_item.shape[0]
    summed = element_item.astype(jnp.float32).reshape(span_length // POOL, POOL, element_item.shape[1]).sum(axis=1)
    return lax.optimization_barrier((summed * (POOL ** -0.5)).astype(jnp.bfloat16))


def attend_block(query_rows, key_set, value_set, valid):
    group_size = QHEADS // KVHEADS
    head_queries = query_rows.reshape(BLOCK, KVHEADS, group_size, HD).transpose(1, 0, 2, 3)
    head_keys = key_set.reshape(-1, KVHEADS, HD).transpose(1, 0, 2)
    head_values = value_set.reshape(-1, KVHEADS, HD).transpose(1, 0, 2)

    def one_head(operands):
        part_q, part_k, part_v = operands
        scores = jnp.einsum("tgd,sd->gts", part_q.astype(jnp.float32), part_k.astype(jnp.float32)) * (HD ** -0.5)
        scores = jnp.where(valid, scores, -jnp.inf)
        highest = jnp.max(scores, axis=2, keepdims=True)
        weights = jnp.exp(scores - highest)
        totals = jnp.sum(weights, axis=2)
        rounded = lax.optimization_barrier(weights.astype(jnp.bfloat16))
        mixed = jnp.einsum("gts,sd->tgd", rounded.astype(jnp.float32), part_v.astype(jnp.float32))
        return (mixed / totals.T[:, :, None]).astype(jnp.bfloat16)

    outputs = lax.map(one_head, (head_queries, head_keys, head_values))
    return outputs.transpose(1, 0, 2, 3).reshape(BLOCK, QHEADS * HD)


def reference(queries, keys, values):
    levels = [(keys, values)]
    for level_index in range(3):
        levels.append((pool_level(levels[-1][0]), pool_level(levels[-1][1])))
    padded = [(jnp.pad(pair[0], ((BLOCK, 2 * BLOCK), (0, 0))), jnp.pad(pair[1], ((BLOCK, 2 * BLOCK), (0, 0)))) for pair in levels[:3]]
    blocks = queries.shape[0] // BLOCK
    top_rows = levels[3][0].shape[0]

    def one_block(fine_index):
        key_parts = []
        value_parts = []
        mask_parts = []
        for level_index in range(3):
            coarse = fine_index // (POOL ** level_index)
            start_row = (coarse * BLOCK).astype(jnp.int32)
            key_parts.append(lax.dynamic_slice_in_dim(padded[level_index][0], start_row, 3 * BLOCK, 0))
            value_parts.append(lax.dynamic_slice_in_dim(padded[level_index][1], start_row, 3 * BLOCK, 0))
            positions = (coarse - 1) * BLOCK + jnp.arange(3 * BLOCK, dtype=jnp.int32)
            mask_parts.append((positions >= 0) & (positions < levels[level_index][0].shape[0]))
        key_parts.append(levels[3][0])
        value_parts.append(levels[3][1])
        mask_parts.append(jnp.ones((top_rows,), dtype=bool))
        query_rows = lax.dynamic_slice_in_dim(queries, (fine_index * BLOCK).astype(jnp.int32), BLOCK, 0)
        return attend_block(query_rows, jnp.concatenate(key_parts, axis=0), jnp.concatenate(value_parts, axis=0), jnp.concatenate(mask_parts, axis=0))

    result = lax.map(one_block, jnp.arange(blocks, dtype=jnp.int32))
    return result.reshape(queries.shape[0], QHEADS * HD)
```

```python
import functools
import math

import jax
import jax.numpy as jnp
from jax import lax
from jax.experimental import pallas as pl
from jax.experimental.pallas import tpu as pltpu
from jax.sharding import PartitionSpec as P

HD = 128
QHEADS = 16
KVHEADS = 4
GROUP = QHEADS // KVHEADS
BLOCK = 128
POOL = 8
WIDTH = KVHEADS * HD
BF16 = jnp.bfloat16
F32 = jnp.float32


def pool_rows(rows):
    count = rows.shape[0]
    out_rows = count // POOL
    row = lax.broadcasted_iota(jnp.int32, (out_rows, count), 0)
    column = lax.broadcasted_iota(jnp.int32, (out_rows, count), 1)
    first = row * POOL
    picks = ((column >= first) & (column < first + POOL)).astype(BF16)
    summed = jnp.dot(picks, rows, preferred_element_type=F32)
    return (summed * POOL ** (-0.5)).astype(BF16)


def fused(n_seq, n_outer, has_top, *refs):
    if has_top:
        q_hbm, k_hbm, v_hbm, top_hbm, o_ref = refs[:5]
        scratch = refs[5:]
    else:
        q_hbm, k_hbm, v_hbm, o_ref = refs[:4]
        top_hbm = None
        scratch = refs[4:]
    (q_ref, kv0, kv1, kv2, kv2f, top, peak, acc, load_sem, halo_send, halo_recv, send1, recv1, send2, recv2) = scratch
    tok = q_ref.shape[0]
    blocks = tok // BLOCK
    n = n_seq * n_outer
    me = lax.axis_index("outer") * n_seq + lax.axis_index("seq")

    def peer(t):
        return {"outer": lax.div(t, n_seq), "seq": lax.rem(t, n_seq)}

    def window(level):
        rows = tok // POOL**level
        span = BLOCK // rows
        held = min(3 * span, n)
        def start(t):
            return jnp.clip((lax.div(t, span) - 1) * span, 0, n - held)
        centre = lax.div(me, span)
        low = jnp.maximum((centre - 1) * span, 0)
        high = jnp.minimum((centre + 2) * span, n)
        return rows, span, held, start, low, high

    rows1, span1, held1, start1, low1, high1 = window(1)
    rows2, span2, held2, start2, low2, high2 = window(2)
    base1, base2 = start1(me), start2(me)

    loads = [
        pltpu.make_async_copy(k_hbm, kv0.at[pl.ds(BLOCK, tok), pl.ds(0, WIDTH)], load_sem.at[0]),
        pltpu.make_async_copy(v_hbm, kv0.at[pl.ds(BLOCK, tok), pl.ds(WIDTH, WIDTH)], load_sem.at[1]),
        pltpu.make_async_copy(q_hbm, q_ref, load_sem.at[2]),
    ]
    if has_top:
        loads.append(pltpu.make_async_copy(top_hbm, top, load_sem.at[3]))
    for load in loads:
        load.start()

    barrier = pltpu.get_barrier_semaphore()

    @pl.loop(0, held2)
    def _(j):
        t = base2 + j

        @pl.when((t >= low2) & (t < high2) & (t != me))
        def _():
            pl.semaphore_signal(barrier, inc=1, device_id=peer(t), device_id_type=pl.DeviceIdType.MESH)

    loads[0].wait()
    loads[1].wait()
    pooled1 = pool_rows(kv0[pl.ds(BLOCK, tok), :])
    pooled2 = pool_rows(pooled1)
    kv1[me - base1] = pooled1
    kv2[me - base2] = pooled2
    pl.semaphore_wait(barrier, high2 - low2 - 1)

    def remote(src, dst, send, recv, t):
        return pltpu.make_async_remote_copy(
            src_ref=src, dst_ref=dst, send_sem=send, recv_sem=recv,
            device_id=peer(t), device_id_type=pl.DeviceIdType.MESH,
        )

    def to_upper():
        return remote(kv0.at[pl.ds(tok, BLOCK)], kv0.at[pl.ds(0, BLOCK)], halo_send.at[0], halo_recv.at[0], me + 1)

    def to_lower():
        return remote(
            kv0.at[pl.ds(BLOCK, BLOCK)], kv0.at[pl.ds(BLOCK + tok, BLOCK)], halo_send.at[1], halo_recv.at[1], me - 1
        )

    @pl.when(me + 1 < n)
    def _():
        to_upper().start()

    @pl.when(me > 0)
    def _():
        to_lower().start()

    def level_copy(buffer, start, send, recv, t, base):
        slot = me - start(t)
        return remote(buffer.at[me - base], buffer.at[slot], send.at[t - base], recv.at[slot], t)

    def level_wait(buffer, send, recv, j, t):
        return remote(buffer.at[j], buffer.at[j], send.at[j], recv.at[j], t)

    def send_level(buffer, start, send, recv, base, held, low, high):
        @pl.loop(0, held)
        def _(j):
            t = base + j

            @pl.when((t >= low) & (t < high) & (t != me))
            def _():
                level_copy(buffer, start, send, recv, t, base).start()

    def recv_level(buffer, send, recv, base, held, low, high):
        @pl.loop(0, held)
        def _(j):
            t = base + j

            @pl.when((t >= low) & (t < high) & (t != me))
            def _():
                level_wait(buffer, send, recv, j, t).wait_recv()

    def sent_level(buffer, send, recv, base, held, low, high):
        @pl.loop(0, held)
        def _(j):
            t = base + j

            @pl.when((t >= low) & (t < high) & (t != me))
            def _():
                level_wait(buffer, send, recv, j, t).wait_send()

    send_level(kv1, start1, send1, recv1, base1, held1, low1, high1)
    send_level(kv2, start2, send2, recv2, base2, held2, low2, high2)

    def fill_level(buffer, own, base, held, low, high):
        blank = jnp.concatenate([own[:, :WIDTH], jnp.zeros_like(own[:, WIDTH:])], axis=1)

        @pl.loop(0, held)
        def _(j):
            t = base + j

            @pl.when((t < low) | (t >= high))
            def _():
                buffer[j] = blank

    if n > 2 * span1:
        fill_level(kv1, pooled1, base1, held1, low1, high1)
    if n > 2 * span2:
        fill_level(kv2, pooled2, base2, held2, low2, high2)

    @pl.when(me == 0)
    def _():
        kv0[pl.ds(0, BLOCK), pl.ds(0, WIDTH)] = kv0[pl.ds(BLOCK, BLOCK), pl.ds(0, WIDTH)]
        kv0[pl.ds(0, BLOCK), pl.ds(WIDTH, WIDTH)] = jnp.zeros((BLOCK, WIDTH), BF16)

    @pl.when(me == n - 1)
    def _():
        kv0[pl.ds(BLOCK + tok, BLOCK), pl.ds(0, WIDTH)] = kv0[pl.ds(tok, BLOCK), pl.ds(0, WIDTH)]
        kv0[pl.ds(BLOCK + tok, BLOCK), pl.ds(WIDTH, WIDTH)] = jnp.zeros((BLOCK, WIDTH), BF16)

    loads[2].wait()
    scale = HD ** (-0.5) * math.log2(math.e)

    def query(h, b):
        parts = []
        for g in range(GROUP):
            column = pl.multiple_of(h * (GROUP * HD) + g * HD, HD)
            parts.append(q_ref[pl.ds(b * BLOCK, BLOCK), pl.ds(column, HD)])
        return jnp.concatenate(parts, axis=0)

    def scored(h, b, parts, first, last):
        q = query(h, b)
        unit = h * blocks + b
        scores = [
            lax.dot_general(q, k, (((1,), (1,)), ((), ())), preferred_element_type=F32) for k, _ in parts
        ]
        highest = jnp.max(scores[0], axis=1, keepdims=True)
        for s in scores[1:]:
            highest = jnp.maximum(highest, jnp.max(s, axis=1, keepdims=True))
        if not first:
            old = peak[unit][:, :1]
            highest = jnp.maximum(highest, old)
        mixed = None
        for s, (_, v) in zip(scores, parts):
            weights = jnp.exp2((s - highest) * scale).astype(BF16)
            term = jnp.dot(weights, v, preferred_element_type=F32)
            mixed = term if mixed is None else mixed + term
        if not first:
            mixed = mixed + acc[unit] * jnp.exp2((old - highest) * scale)
        if not last:
            peak[unit] = jnp.broadcast_to(highest, (GROUP * BLOCK, HD))
            acc[unit] = mixed
            return
        out = (mixed[:, :HD] / mixed[:, HD:]).astype(BF16)
        for g in range(GROUP):
            column = pl.multiple_of(h * (GROUP * HD) + g * HD, HD)
            o_ref[pl.ds(b * BLOCK, BLOCK), pl.ds(column, HD)] = out[g * BLOCK : (g + 1) * BLOCK]

    def head_columns(h):
        return pl.multiple_of(h * HD, HD), pl.multiple_of(WIDTH + h * HD, HD)

    def with_count(v, count):
        return jnp.concatenate([v, count], axis=1)

    def counts(rows, low, high):
        row = lax.broadcasted_iota(jnp.int32, (rows, HD), 0)
        return ((row >= low) & (row < high)).astype(F32).astype(BF16)

    def fine(h, start, size, present):
        key_column, value_column = head_columns(h)
        k = kv0[pl.ds(start, size), pl.ds(key_column, HD)]
        v = kv0[pl.ds(start, size), pl.ds(value_column, HD)]
        count = jnp.ones((size, HD), BF16) if present is None else counts(size, 0, jnp.where(present, size, 0))
        return k, with_count(v, count)

    @pl.loop(0, KVHEADS)
    def _(h):
        for b in range(blocks):
            low, high = max(b, 1), min(b + 2, blocks)
            scored(h, b, [fine(h, low * BLOCK, (high - low + 1) * BLOCK, None)], True, False)

    @pl.when(me > 0)
    def _():
        to_upper().wait_recv()

    @pl.when(me + 1 < n)
    def _():
        to_lower().wait_recv()

    recv_level(kv1, send1, recv1, base1, held1, low1, high1)

    @pl.loop(0, KVHEADS)
    def _(h):
        key_column, value_column = head_columns(h)
        k1 = kv1[:, :, pl.ds(key_column, HD)].reshape(held1 * rows1, HD)
        v1 = kv1[:, :, pl.ds(value_column, HD)].reshape(held1 * rows1, HD)
        coarse = (k1, with_count(v1, counts(held1 * rows1, (low1 - base1) * rows1, (high1 - base1) * rows1)))
        for b in range(blocks):
            parts = [coarse]
            if b == 0:
                parts.append(fine(h, 0, BLOCK, me > 0))
            if b == blocks - 1:
                parts.append(fine(h, BLOCK + tok, BLOCK, me < n - 1))
            scored(h, b, parts, False, False)

    recv_level(kv2, send2, recv2, base2, held2, low2, high2)
    kv2f[...] = kv2[...].astype(F32).reshape(held2 * rows2, 2 * WIDTH).astype(BF16)
    if not has_top:
        top[...] = pool_rows(kv2f[...])
    else:
        loads[3].wait()

    @pl.loop(0, KVHEADS)
    def _(h):
        key_column, value_column = head_columns(h)
        k2 = kv2f[:, pl.ds(key_column, HD)]
        v2 = kv2f[:, pl.ds(value_column, HD)]
        count2 = counts(held2 * rows2, (low2 - base2) * rows2, (high2 - base2) * rows2)
        k3 = top[:, pl.ds(key_column, HD)]
        v3 = top[:, pl.ds(value_column, HD)]
        parts = [(k2, with_count(v2, count2)), (k3, with_count(v3, jnp.ones((v3.shape[0], HD), BF16)))]
        for b in range(blocks):
            scored(h, b, parts, False, True)

    @pl.when(me + 1 < n)
    def _():
        to_upper().wait_send()

    @pl.when(me > 0)
    def _():
        to_lower().wait_send()

    sent_level(kv1, send1, recv1, base1, held1, low1, high1)
    sent_level(kv2, send2, recv2, base2, held2, low2, high2)


def pool_level(rows):
    summed = rows.astype(F32).reshape(rows.shape[0] // POOL, POOL, rows.shape[1]).sum(axis=1)
    return (summed * POOL ** (-0.5)).astype(BF16)


def local(n_seq, n_outer, queries, keys, values):
    tok = queries.shape[0]
    n = n_seq * n_outer
    rows1, rows2 = tok // POOL, tok // POOL**2
    held1 = min(3 * (BLOCK // rows1), n)
    held2 = min(3 * (BLOCK // rows2), n)
    has_top = held2 < n
    operands = [queries, keys, values]
    if has_top:
        joined = jnp.concatenate([keys, values], axis=1)
        own = pool_level(pool_level(pool_level(joined)))
        operands.append(lax.all_gather(own, ("outer", "seq"), axis=0, tiled=True))
    top_rows = n * tok // POOL**3
    units = KVHEADS * (tok // BLOCK)
    return pl.pallas_call(
        functools.partial(fused, n_seq, n_outer, has_top),
        out_shape=jax.ShapeDtypeStruct((tok, QHEADS * HD), BF16),
        in_specs=[pl.BlockSpec(memory_space=pl.ANY)] * len(operands),
        out_specs=pl.BlockSpec(memory_space=pltpu.VMEM),
        scratch_shapes=[
            pltpu.VMEM((tok, QHEADS * HD), BF16),
            pltpu.VMEM((tok + 2 * BLOCK, 2 * WIDTH), BF16),
            pltpu.VMEM((held1, rows1, 2 * WIDTH), BF16),
            pltpu.VMEM((held2, rows2, 2 * WIDTH), BF16),
            pltpu.VMEM((held2 * rows2, 2 * WIDTH), BF16),
            pltpu.VMEM((top_rows, 2 * WIDTH), BF16),
            pltpu.VMEM((units, GROUP * BLOCK, HD), F32),
            pltpu.VMEM((units, GROUP * BLOCK, 2 * HD), F32),
            pltpu.SemaphoreType.DMA((4,)),
            pltpu.SemaphoreType.DMA((2,)),
            pltpu.SemaphoreType.DMA((2,)),
            pltpu.SemaphoreType.DMA((held1,)),
            pltpu.SemaphoreType.DMA((held1,)),
            pltpu.SemaphoreType.DMA((held2,)),
            pltpu.SemaphoreType.DMA((held2,)),
        ],
        compiler_params=pltpu.CompilerParams(
            collective_id=0, has_side_effects=True, vmem_limit_bytes=56 * 1024 * 1024
        ),
    )(*operands)


def solution(mesh):
    spec = P(("outer", "seq"), None)
    return jax.shard_map(
        functools.partial(local, mesh.shape["seq"], mesh.shape["outer"]),
        mesh=mesh,
        in_specs=(spec, spec, spec),
        out_specs=spec,
        check_vma=False,
    )
```

```python
import functools
import math

import jax
import jax.numpy as jnp
from jax import lax
from jax.experimental import pallas as pl
from jax.experimental.pallas import tpu as pltpu
from jax.sharding import PartitionSpec as P

HD = 128
QHEADS = 16
KVHEADS = 4
GROUP = QHEADS // KVHEADS
BLOCK = 128
POOL = 8
WIDTH = KVHEADS * HD
BF16 = jnp.bfloat16
F32 = jnp.float32


def pool_rows(rows):
    count = rows.shape[0]
    out_rows = count // POOL
    row = lax.broadcasted_iota(jnp.int32, (out_rows, count), 0)
    column = lax.broadcasted_iota(jnp.int32, (out_rows, count), 1)
    first = row * POOL
    picks = ((column >= first) & (column < first + POOL)).astype(BF16)
    summed = jnp.dot(picks, rows, preferred_element_type=F32)
    return (summed * POOL ** (-0.5)).astype(BF16)


def fused(n_seq, n_outer, spread, *refs):
    if spread:
        q_hbm, k_hbm, v_hbm, o_ref = refs[:4]
        top_hbm = None
        scratch = refs[4:]
    else:
        q_hbm, k_hbm, v_hbm, top_hbm, o_ref = refs[:5]
        scratch = refs[5:]
    (q_ref, kv0, kvc, kv2, peak, acc, load_sem, halo_send, halo_recv, send1, recv1, send2, recv2) = scratch
    tok = q_ref.shape[0]
    blocks = tok // BLOCK
    n = n_seq * n_outer
    rows1, rows2 = tok // POOL, tok // POOL**2
    span2 = BLOCK // rows2
    held2 = kv2.shape[0] * kv2.shape[1]
    pair = 2 * rows1
    level1 = 3 * BLOCK
    level2 = held2 * rows2
    top_rows = n * tok // POOL**3
    me = lax.axis_index("outer") * n_seq + lax.axis_index("seq")
    odd = lax.rem(me, 2)
    last_pair = n // 2 - 1
    a = lax.div(me, 2)
    phase = lax.rem(a, 4)
    a_odd = lax.rem(a, 2)

    def peer(t):
        return {"outer": lax.div(t, n_seq), "seq": lax.rem(t, n_seq)}

    def flipped(bit):
        return me + bit - 2 * bit * lax.rem(lax.div(me, bit), 2)

    def remote(src, dst, send, recv, t):
        return pltpu.make_async_remote_copy(
            src_ref=src, dst_ref=dst, send_sem=send, recv_sem=recv,
            device_id=peer(t), device_id_type=pl.DeviceIdType.MESH,
        )

    centre2 = lax.div(me, span2)
    low2 = jnp.maximum((centre2 - 1) * span2, 0)
    high2 = jnp.minimum((centre2 + 2) * span2, n)

    def start2(t):
        return jnp.clip((lax.div(t, span2) - 1) * span2, 0, n - held2)

    base2 = start2(me)

    loads = [
        pltpu.make_async_copy(k_hbm, kv0.at[pl.ds(BLOCK, tok), pl.ds(0, WIDTH)], load_sem.at[0]),
        pltpu.make_async_copy(v_hbm, kv0.at[pl.ds(BLOCK, tok), pl.ds(WIDTH, WIDTH)], load_sem.at[1]),
        pltpu.make_async_copy(q_hbm, q_ref, load_sem.at[2]),
    ]
    top_at = level1 + level2
    if not spread:
        loads.append(pltpu.make_async_copy(top_hbm, kvc.at[pl.ds(top_at, top_rows)], load_sem.at[3]))
    for load in loads:
        load.start()

    across = me - 1 + 2 * odd
    has_across = (across >= 0) & (across < n)
    cross_up = (phase == 3) & (a < last_pair)
    cross_down = (phase == 0) & (a > 0)

    barrier = pltpu.get_barrier_semaphore()

    def greet(t):
        pl.semaphore_signal(barrier, inc=1, device_id=peer(t), device_id_type=pl.DeviceIdType.MESH)

    if spread:
        bits = []
        bit = POOL
        while bit < n:
            bits.append(bit)
            bit *= 2
        bits += [1, 2, 4]
        for bit in bits:
            greet(flipped(bit))
        pl.when(has_across)(lambda: greet(across))
        pl.when(cross_up)(lambda: greet(me + 2))
        pl.when(cross_down)(lambda: greet(me - 2))
        met = len(bits) + has_across.astype(jnp.int32) + (cross_up | cross_down).astype(jnp.int32)
    else:
        @pl.loop(0, held2)
        def _(j):
            t = base2 + j
            pl.when((t >= low2) & (t < high2) & (t != me))(lambda: greet(t))

        met = high2 - low2 - 1

    loads[0].wait()
    loads[1].wait()
    pooled1 = pool_rows(kv0[pl.ds(BLOCK, tok), :])
    own1 = pl.multiple_of(pair + odd * rows1, rows1)
    kvc[pl.ds(own1, rows1), :] = pooled1
    pooled2 = pool_rows(pooled1)
    slot = me - base2
    kv2[lax.div(slot, POOL), lax.rem(slot, POOL)] = pooled2
    pl.semaphore_wait(barrier, met)

    def pair_at(start):
        return kvc.at[pl.ds(pl.multiple_of(start, pair), pair)]

    def half_copy():
        rows = kvc.at[pl.ds(own1, rows1)]
        return remote(rows, rows, send1.at[0], recv1.at[0], flipped(1))

    def half_wait():
        rows = kvc.at[pl.ds(pl.multiple_of(pair + (1 - odd) * rows1, rows1), rows1)]
        return remote(rows, rows, send1.at[0], recv1.at[0], flipped(1))

    def swap_copy():
        return remote(pair_at(pair), pair_at(a_odd * (2 * pair)), send1.at[1], recv1.at[1], flipped(2))

    def swap_wait():
        rows = pair_at((1 - a_odd) * (2 * pair))
        return remote(rows, rows, send1.at[1], recv1.at[1], flipped(2))

    def cross_copy(up):
        return remote(
            pair_at(pair), pair_at(0 if up else 2 * pair), send1.at[2], recv1.at[2], me + 2 if up else me - 2
        )

    def pass_copy(up):
        return remote(
            pair_at(2 * pair if up else 0), pair_at(0 if up else 2 * pair), send1.at[3], recv1.at[2],
            me + 4 if up else me - 4,
        )

    def third_wait():
        rows = pair_at(a_odd * (2 * pair))
        return remote(rows, rows, send1.at[2], recv1.at[2], flipped(4))

    has_third = (phase == 1) | (phase == 2) | cross_up | cross_down

    def halo_copy(up):
        if up:
            return remote(kv0.at[pl.ds(tok, BLOCK)], kv0.at[pl.ds(0, BLOCK)], halo_send.at[0], halo_recv.at[0], me + 1)
        return remote(
            kv0.at[pl.ds(BLOCK, BLOCK)], kv0.at[pl.ds(BLOCK + tok, BLOCK)], halo_send.at[1], halo_recv.at[1], me - 1
        )

    def halo_start(wanted):
        pl.when((me + 1 < n) & (odd == (1 - wanted)))(lambda: halo_copy(True).start())
        pl.when((me > 0) & (odd == wanted))(lambda: halo_copy(False).start())

    if spread:
        def region(step, whose):
            bit = bits[step]
            flips = lax.rem(lax.div(me, bit), 2)
            at = me if whose == 0 else me + bit - 2 * bit * flips
            k, l = lax.div(at, POOL), lax.rem(at, POOL)
            if bit >= POOL:
                size = bit // POOL
                return kv2.at[pl.ds(lax.div(k, size) * size, size), pl.ds(l, 1)]
            return kv2.at[:, pl.ds(lax.div(l, bit) * bit, bit)]

        def step_copy(step):
            rows = region(step, 0)
            return remote(rows, rows, send2.at[step], recv2.at[step], flipped(bits[step]))

        def step_wait(step):
            rows = region(step, 1)
            return remote(rows, rows, send2.at[step], recv2.at[step], flipped(bits[step]))
    else:
        def over_window(act):
            @pl.loop(0, held2)
            def _(j):
                t = base2 + j
                pl.when((t >= low2) & (t < high2) & (t != me))(lambda: act(j, t))

        def slot_at(j):
            return kv2.at[lax.div(j, POOL), lax.rem(j, POOL)]

        def direct_copy(j, t):
            there = me - start2(t)
            remote(slot_at(slot), slot_at(there), send2.at[j], recv2.at[there], t).start()

        def direct_wait(j, t):
            return remote(slot_at(j), slot_at(j), send2.at[j], recv2.at[j], t)

    half_copy().start()
    if spread:
        step_copy(0).start()

    def blank_of(own):
        return jnp.concatenate([own[:, :WIDTH], jnp.zeros_like(own[:, WIDTH:])], axis=1)

    blank1 = jnp.concatenate([blank_of(pooled1)] * 2, axis=0)

    @pl.when(a == 0)
    def _():
        kvc[pl.ds(0, pair), :] = blank1

    @pl.when(a == last_pair)
    def _():
        kvc[pl.ds(2 * pair, pair), :] = blank1

    if n > 2 * span2:
        blank2 = blank_of(pooled2)

        @pl.loop(0, held2)
        def _(j):
            t = base2 + j

            @pl.when((t < low2) | (t >= high2))
            def _():
                kv2[lax.div(j, POOL), lax.rem(j, POOL)] = blank2

    @pl.when(me == 0)
    def _():
        kv0[pl.ds(0, BLOCK), :] = blank_of(kv0[pl.ds(BLOCK, BLOCK), :])

    @pl.when(me == n - 1)
    def _():
        kv0[pl.ds(BLOCK + tok, BLOCK), :] = blank_of(kv0[pl.ds(tok, BLOCK), :])

    loads[2].wait()
    scale = HD ** (-0.5) * math.log2(math.e)

    def query(h, b):
        parts = []
        for g in range(GROUP):
            column = pl.multiple_of(h * (GROUP * HD) + g * HD, HD)
            parts.append(q_ref[pl.ds(b * BLOCK, BLOCK), pl.ds(column, HD)])
        return jnp.concatenate(parts, axis=0)

    def across_lanes(x, width):
        if width % HD == 0:
            return jnp.concatenate([x] * (width // HD), axis=1)
        whole = [x] * (width // HD) + [x[:, : width % HD]]
        return jnp.concatenate(whole, axis=1)

    def scored(h, b, k, v, first, last):
        q = query(h, b)
        unit = h * blocks + b
        s = lax.dot_general(q, k, (((1,), (1,)), ((), ())), preferred_element_type=F32)
        highest = jnp.broadcast_to(jnp.max(s, axis=1, keepdims=True), (GROUP * BLOCK, HD))
        if not first:
            old = peak[unit]
            highest = jnp.maximum(highest, old)
        weights = jnp.exp2((s - across_lanes(highest, s.shape[1])) * scale).astype(BF16)
        mixed = jnp.dot(weights, v, preferred_element_type=F32)
        if not first:
            keep = jnp.exp2((old - highest) * scale)
            mixed = mixed + acc[unit] * across_lanes(keep, 2 * HD)
        if not last:
            peak[unit] = highest
            acc[unit] = mixed
            return
        out = (mixed[:, :HD] / mixed[:, HD:]).astype(BF16)
        for g in range(GROUP):
            column = pl.multiple_of(h * (GROUP * HD) + g * HD, HD)
            o_ref[pl.ds(b * BLOCK, BLOCK), pl.ds(column, HD)] = out[g * BLOCK : (g + 1) * BLOCK]

    def head_columns(h):
        return pl.multiple_of(h * HD, HD), pl.multiple_of(WIDTH + h * HD, HD)

    def fine(h, start, size, present):
        key_column, value_column = head_columns(h)
        k = kv0[pl.ds(start, size), pl.ds(key_column, HD)]
        v = kv0[pl.ds(start, size), pl.ds(value_column, HD)]
        if present is None:
            count = jnp.ones((size, HD), BF16)
        else:
            row = lax.broadcasted_iota(jnp.int32, (size, HD), 0)
            count = (row < jnp.where(present, size, 0)).astype(F32).astype(BF16)
        return k, jnp.concatenate([v, count], axis=1)

    def own_rows(h):
        for b in range(blocks):
            low, high = max(b, 1), min(b + 2, blocks)
            scored(h, b, *fine(h, low * BLOCK, (high - low + 1) * BLOCK, None), True, False)

    def own_loop(low, high):
        @pl.loop(low, high)
        def _(h):
            own_rows(h)

    if spread:
        zs = len(bits) - 3
        at = 0
        for z in range(zs):
            stop = at + 1 if at < KVHEADS else at
            own_loop(at, stop)
            at = stop
            step_wait(z).wait_recv()
            step_copy(z + 1).start()
        half_wait().wait_recv()
        swap_copy().start()
        pl.when(cross_up)(lambda: cross_copy(True).start())
        pl.when(cross_down)(lambda: cross_copy(False).start())
        halo_start(1)
        stop = max(at, KVHEADS - 1)
        own_loop(at, stop)
        step_wait(zs).wait_recv()
        step_copy(zs + 1).start()
        halo_start(0)
        own_loop(stop, KVHEADS)
    else:
        over_window(direct_copy)
        half_wait().wait_recv()
        swap_copy().start()
        pl.when(cross_up)(lambda: cross_copy(True).start())
        pl.when(cross_down)(lambda: cross_copy(False).start())
        halo_start(1)
        halo_start(0)
        own_loop(0, KVHEADS)

    swap_wait().wait_recv()
    pl.when(phase == 0)(lambda: pass_copy(True).start())
    pl.when(phase == 3)(lambda: pass_copy(False).start())
    if spread:
        step_wait(zs + 1).wait_recv()
        step_copy(zs + 2).start()
        step_wait(zs + 2).wait_recv()
    else:
        over_window(lambda j, t: direct_wait(j, t).wait_recv())
    second = kv2[...].astype(F32).reshape(level2, 2 * WIDTH).astype(BF16)
    kvc[pl.ds(level1, level2), :] = second
    if spread:
        kvc[pl.ds(top_at, top_rows), :] = pool_rows(second)
    else:
        loads[3].wait()
    pl.when(has_third)(lambda: third_wait().wait_recv())

    coarse_rows = level1 + level2 + top_rows
    row = lax.broadcasted_iota(jnp.int32, (coarse_rows, HD), 0)
    missing = ((row < jnp.where(a == 0, pair, 0))) | (
        (row >= jnp.where(a == last_pair, 2 * pair, level1)) & (row < level1)
    )
    if n > 2 * span2:
        missing = missing | (
            (row >= level1) & (row < top_at)
            & ((row < level1 + (low2 - base2) * rows2) | (row >= level1 + (high2 - base2) * rows2))
        )
    coarse_count = jnp.where(missing, 0.0, 1.0).astype(BF16)

    @pl.loop(0, KVHEADS)
    def _(h):
        key_column, value_column = head_columns(h)
        k = kvc[:, pl.ds(key_column, HD)]
        v = jnp.concatenate([kvc[:, pl.ds(value_column, HD)], coarse_count], axis=1)
        for b in range(blocks):
            scored(h, b, k, v, False, 0 < b < blocks - 1)

    pl.when(me > 0)(lambda: halo_copy(True).wait_recv())
    pl.when(me + 1 < n)(lambda: halo_copy(False).wait_recv())

    @pl.loop(0, KVHEADS)
    def _(h):
        scored(h, 0, *fine(h, 0, BLOCK, me > 0), False, blocks > 1)
        scored(h, blocks - 1, *fine(h, BLOCK + tok, BLOCK, me < n - 1), False, True)

    pl.when(me + 1 < n)(lambda: halo_copy(True).wait_send())
    pl.when(me > 0)(lambda: halo_copy(False).wait_send())
    half_copy().wait_send()
    swap_copy().wait_send()
    pl.when(cross_up)(lambda: cross_copy(True).wait_send())
    pl.when(cross_down)(lambda: cross_copy(False).wait_send())
    pl.when(phase == 0)(lambda: pass_copy(True).wait_send())
    pl.when(phase == 3)(lambda: pass_copy(False).wait_send())
    if spread:
        for step in range(len(bits)):
            step_copy(step).wait_send()
    else:
        over_window(lambda j, t: direct_wait(j, t).wait_send())


def pool_level(rows):
    summed = rows.astype(F32).reshape(rows.shape[0] // POOL, POOL, rows.shape[1]).sum(axis=1)
    return (summed * POOL ** (-0.5)).astype(BF16)


def local(n_seq, n_outer, queries, keys, values):
    tok = queries.shape[0]
    n = n_seq * n_outer
    rows1, rows2 = tok // POOL, tok // POOL**2
    assert 2 * rows1 == BLOCK and n % 8 == 0
    held2 = min(3 * (BLOCK // rows2), n)
    spread = held2 == n and n & (n - 1) == 0
    operands = [queries, keys, values]
    if not spread:
        joined = jnp.concatenate([keys, values], axis=1)
        own = pool_level(pool_level(pool_level(joined)))
        operands.append(lax.all_gather(own, ("outer", "seq"), axis=0, tiled=True))
    coarse_rows = 3 * BLOCK + held2 * rows2 + n * tok // POOL**3
    units = KVHEADS * (tok // BLOCK)
    return pl.pallas_call(
        functools.partial(fused, n_seq, n_outer, spread),
        out_shape=jax.ShapeDtypeStruct((tok, QHEADS * HD), BF16),
        in_specs=[pl.BlockSpec(memory_space=pltpu.HBM)] * len(operands),
        out_specs=pl.BlockSpec(memory_space=pltpu.VMEM),
        scratch_shapes=[
            pltpu.VMEM((tok, QHEADS * HD), BF16),
            pltpu.VMEM((tok + 2 * BLOCK, 2 * WIDTH), BF16),
            pltpu.VMEM((coarse_rows, 2 * WIDTH), BF16),
            pltpu.VMEM((held2 // POOL, POOL, rows2, 2 * WIDTH), BF16),
            pltpu.VMEM((units, GROUP * BLOCK, HD), F32),
            pltpu.VMEM((units, GROUP * BLOCK, 2 * HD), F32),
            pltpu.SemaphoreType.DMA((4,)),
            pltpu.SemaphoreType.DMA((2,)),
            pltpu.SemaphoreType.DMA((2,)),
            pltpu.SemaphoreType.DMA((4,)),
            pltpu.SemaphoreType.DMA((3,)),
            pltpu.SemaphoreType.DMA((held2,)),
            pltpu.SemaphoreType.DMA((held2,)),
        ],
        compiler_params=pltpu.CompilerParams(
            collective_id=0, has_side_effects=True, vmem_limit_bytes=44 * 1024 * 1024
        ),
    )(*operands)


def solution(mesh):
    spec = P(("outer", "seq"), None)
    return jax.shard_map(
        functools.partial(local, mesh.shape["seq"], mesh.shape["outer"]),
        mesh=mesh,
        in_specs=(spec, spec, spec),
        out_specs=spec,
        check_vma=False,
    )
```

```python
import functools
import math

import jax
import jax.numpy as jnp
from jax import lax
from jax.experimental import pallas as pl
from jax.experimental.pallas import tpu as pltpu
from jax.sharding import PartitionSpec as P

HD = 128
QHEADS = 16
KVHEADS = 4
GROUP = QHEADS // KVHEADS
BLOCK = 128
POOL = 8
WIDTH = KVHEADS * HD
PER_HEAD = 2 * HD
CHUNKS = 2
CHUNK = 2 * WIDTH // CHUNKS
BF16 = jnp.bfloat16
F32 = jnp.float32


def pool_rows(rows):
    count = rows.shape[0]
    out_rows = count // POOL
    row = lax.broadcasted_iota(jnp.int32, (out_rows, count), 0)
    column = lax.broadcasted_iota(jnp.int32, (out_rows, count), 1)
    first = row * POOL
    picks = ((column >= first) & (column < first + POOL)).astype(BF16)
    summed = jnp.dot(picks, rows, preferred_element_type=F32)
    return (summed * POOL ** (-0.5)).astype(BF16)


def fused(n_seq, n_outer, spread, *refs):
    if spread:
        q_hbm, k_hbm, v_hbm, o_ref = refs[:4]
        top_hbm = None
        scratch = refs[4:]
    else:
        q_hbm, k_hbm, v_hbm, top_hbm, o_ref = refs[:5]
        scratch = refs[5:]
    (q_ref, kv0, kvc, kv2, peak, acc, load_sem, halo_send, halo_recv, send1, recv1, send2, recv2) = scratch
    tok = q_ref.shape[0]
    blocks = tok // BLOCK
    n = n_seq * n_outer
    rows1, rows2 = tok // POOL, tok // POOL**2
    span2 = BLOCK // rows2
    held2 = kv2.shape[0] * kv2.shape[1]
    pair = 2 * rows1
    level1 = 3 * BLOCK
    level2 = held2 * rows2
    top_rows = n * tok // POOL**3
    me = lax.axis_index("outer") * n_seq + lax.axis_index("seq")
    odd = lax.rem(me, 2)
    last_pair = n // 2 - 1
    a = lax.div(me, 2)
    phase = lax.rem(a, 4)
    a_odd = lax.rem(a, 2)

    def peer(t):
        return {"outer": lax.div(t, n_seq), "seq": lax.rem(t, n_seq)}

    def flipped(bit):
        return me + bit - 2 * bit * lax.rem(lax.div(me, bit), 2)

    def remote(src, dst, send, recv, t):
        return pltpu.make_async_remote_copy(
            src_ref=src, dst_ref=dst, send_sem=send, recv_sem=recv,
            device_id=peer(t), device_id_type=pl.DeviceIdType.MESH,
        )

    centre2 = lax.div(me, span2)
    low2 = jnp.maximum((centre2 - 1) * span2, 0)
    high2 = jnp.minimum((centre2 + 2) * span2, n)

    def start2(t):
        return jnp.clip((lax.div(t, span2) - 1) * span2, 0, n - held2)

    base2 = start2(me)

    loads = []
    for h in range(KVHEADS):
        for part, source in enumerate((k_hbm, v_hbm)):
            columns = pl.ds(h * PER_HEAD + part * HD, HD)
            loads.append(
                pltpu.make_async_copy(
                    source.at[:, pl.ds(h * HD, HD)], kv0.at[pl.ds(BLOCK, tok), columns], load_sem.at[len(loads)]
                )
            )
    own_loads = list(loads)
    q_load = pltpu.make_async_copy(q_hbm, q_ref, load_sem.at[2 * KVHEADS])
    loads.append(q_load)
    top_at = level1 + level2
    if not spread:
        loads.append(pltpu.make_async_copy(top_hbm, kvc.at[pl.ds(top_at, top_rows)], load_sem.at[2 * KVHEADS + 1]))
    for load in loads:
        load.start()

    across = me - 1 + 2 * odd
    has_across = (across >= 0) & (across < n)
    cross_up = (phase == 3) & (a < last_pair)
    cross_down = (phase == 0) & (a > 0)

    barrier = pltpu.get_barrier_semaphore()

    def greet(t):
        pl.semaphore_signal(barrier, inc=1, device_id=peer(t), device_id_type=pl.DeviceIdType.MESH)

    if spread:
        bits = []
        bit = POOL
        while bit < n:
            bits.append(bit)
            bit *= 2
        bits += [2, 1, 4]
        for bit in bits:
            greet(flipped(bit))
        pl.when(has_across)(lambda: greet(across))
        pl.when(cross_up)(lambda: greet(me + 2))
        pl.when(cross_down)(lambda: greet(me - 2))
        met = len(bits) + has_across.astype(jnp.int32) + (cross_up | cross_down).astype(jnp.int32)
    else:
        @pl.loop(0, held2)
        def _(j):
            t = base2 + j
            pl.when((t >= low2) & (t < high2) & (t != me))(lambda: greet(t))

        met = high2 - low2 - 1

    for load in own_loads:
        load.wait()
    pooled1 = pool_rows(kv0[pl.ds(BLOCK, tok), :])
    own1 = pl.multiple_of(pair + odd * rows1, rows1)
    kvc[pl.ds(own1, rows1), :] = pooled1
    pooled2 = pool_rows(pooled1)
    slot = me - base2

    def inner(t):
        low = lax.rem(t, POOL)
        if not spread:
            return low
        return lax.rem(low, 2) * 2 + lax.rem(lax.div(low, 2), 2) + lax.div(low, 4) * 4

    kv2[lax.div(slot, POOL), inner(slot)] = pooled2
    pl.semaphore_wait(barrier, met)

    def columns_of(c):
        return pl.ds(c * CHUNK, CHUNK)

    def pair_at(start, c):
        return kvc.at[pl.ds(pl.multiple_of(start, pair), pair), columns_of(c)]

    def half_copy(c):
        rows = kvc.at[pl.ds(own1, rows1), columns_of(c)]
        return remote(rows, rows, send1.at[c, 0], recv1.at[c, 0], flipped(1))

    def half_wait(c):
        rows = kvc.at[pl.ds(pl.multiple_of(pair + (1 - odd) * rows1, rows1), rows1), columns_of(c)]
        return remote(rows, rows, send1.at[c, 0], recv1.at[c, 0], flipped(1))

    def swap_copy(c):
        return remote(
            pair_at(pair, c), pair_at(a_odd * (2 * pair), c), send1.at[c, 1], recv1.at[c, 1], flipped(2)
        )

    def swap_wait(c):
        rows = pair_at((1 - a_odd) * (2 * pair), c)
        return remote(rows, rows, send1.at[c, 1], recv1.at[c, 1], flipped(2))

    def cross_copy(up, c):
        return remote(
            pair_at(pair, c), pair_at(0 if up else 2 * pair, c), send1.at[c, 2], recv1.at[c, 2],
            me + 2 if up else me - 2,
        )

    def pass_copy(up, c):
        return remote(
            pair_at(2 * pair if up else 0, c), pair_at(0 if up else 2 * pair, c), send1.at[c, 3], recv1.at[c, 2],
            me + 4 if up else me - 4,
        )

    def third_wait(c):
        rows = pair_at(a_odd * (2 * pair), c)
        return remote(rows, rows, send1.at[c, 2], recv1.at[c, 2], flipped(4))

    has_third = (phase == 1) | (phase == 2) | cross_up | cross_down

    def halo_copy(up, c):
        columns = columns_of(c)
        if up:
            return remote(
                kv0.at[pl.ds(tok, BLOCK), columns], kv0.at[pl.ds(0, BLOCK), columns],
                halo_send.at[c, 0], halo_recv.at[c, 0], me + 1,
            )
        return remote(
            kv0.at[pl.ds(BLOCK, BLOCK), columns], kv0.at[pl.ds(BLOCK + tok, BLOCK), columns],
            halo_send.at[c, 1], halo_recv.at[c, 1], me - 1,
        )

    def halo_start(wanted, c):
        pl.when((me + 1 < n) & (odd == (1 - wanted)))(lambda: halo_copy(True, c).start())
        pl.when((me > 0) & (odd == wanted))(lambda: halo_copy(False, c).start())

    if spread:
        def region(step, whose, c):
            bit = bits[step]
            flips = lax.rem(lax.div(me, bit), 2)
            at = me if whose == 0 else me + bit - 2 * bit * flips
            k, l = lax.div(at, POOL), inner(at)
            if bit >= POOL:
                size = bit // POOL
                return kv2.at[pl.ds(lax.div(k, size) * size, size), pl.ds(l, 1), :, columns_of(c)]
            size = {2: 1, 1: 2, 4: 4}[bit]
            return kv2.at[:, pl.ds(lax.div(l, size) * size, size), :, columns_of(c)]

        def step_copy(step, c):
            rows = region(step, 0, c)
            return remote(rows, rows, send2.at[c, step], recv2.at[c, step], flipped(bits[step]))

        def step_wait(step, c):
            rows = region(step, 1, c)
            return remote(rows, rows, send2.at[c, step], recv2.at[c, step], flipped(bits[step]))
    else:
        def over_window(act):
            @pl.loop(0, held2)
            def _(j):
                t = base2 + j
                pl.when((t >= low2) & (t < high2) & (t != me))(lambda: act(j, t))

        def slot_at(j):
            return kv2.at[lax.div(j, POOL), lax.rem(j, POOL)]

        def direct_copy(j, t):
            there = me - start2(t)
            remote(slot_at(slot), slot_at(there), send2.at[0, j], recv2.at[0, there], t).start()

        def direct_wait(j, t):
            return remote(slot_at(j), slot_at(j), send2.at[0, j], recv2.at[0, j], t)

    for c in range(CHUNKS):
        half_copy(c).start()
        if spread:
            step_copy(0, c).start()

    def blank_of(own):
        parts = []
        for h in range(KVHEADS):
            keys = own[:, h * PER_HEAD : h * PER_HEAD + HD]
            parts += [keys, jnp.zeros_like(keys)]
        return jnp.concatenate(parts, axis=1)

    blank1 = jnp.concatenate([blank_of(pooled1)] * 2, axis=0)

    @pl.when(a == 0)
    def _():
        kvc[pl.ds(0, pair), :] = blank1

    @pl.when(a == last_pair)
    def _():
        kvc[pl.ds(2 * pair, pair), :] = blank1

    if n > 2 * span2:
        blank2 = blank_of(pooled2)

        @pl.loop(0, held2)
        def _(j):
            t = base2 + j

            @pl.when((t < low2) | (t >= high2))
            def _():
                kv2[lax.div(j, POOL), lax.rem(j, POOL)] = blank2

    @pl.when(me == 0)
    def _():
        kv0[pl.ds(0, BLOCK), :] = blank_of(kv0[pl.ds(BLOCK, BLOCK), :])

    @pl.when(me == n - 1)
    def _():
        kv0[pl.ds(BLOCK + tok, BLOCK), :] = blank_of(kv0[pl.ds(tok, BLOCK), :])

    q_load.wait()
    scale = HD ** (-0.5) * math.log2(math.e)

    def query(h, b):
        parts = []
        for g in range(GROUP):
            column = pl.multiple_of(h * (GROUP * HD) + g * HD, HD)
            parts.append(q_ref[pl.ds(b * BLOCK, BLOCK), pl.ds(column, HD)])
        return jnp.concatenate(parts, axis=0)

    def across_lanes(x, width):
        if width % HD == 0:
            return jnp.concatenate([x] * (width // HD), axis=1)
        whole = [x] * (width // HD) + [x[:, : width % HD]]
        return jnp.concatenate(whole, axis=1)

    def scored(h, b, k, v, first, last):
        q = query(h, b)
        unit = h * blocks + b
        s = lax.dot_general(q, k, (((1,), (1,)), ((), ())), preferred_element_type=F32)
        highest = jnp.broadcast_to(jnp.max(s, axis=1, keepdims=True), (GROUP * BLOCK, HD))
        if not first:
            old = peak[unit]
            highest = jnp.maximum(highest, old)
        weights = jnp.exp2((s - across_lanes(highest, s.shape[1])) * scale).astype(BF16)
        mixed = jnp.dot(weights, v, preferred_element_type=F32)
        if not first:
            keep = jnp.exp2((old - highest) * scale)
            mixed = mixed + acc[unit] * across_lanes(keep, 2 * HD)
        if not last:
            peak[unit] = highest
            acc[unit] = mixed
            return
        out = (mixed[:, :HD] / mixed[:, HD:]).astype(BF16)
        for g in range(GROUP):
            column = pl.multiple_of(h * (GROUP * HD) + g * HD, HD)
            o_ref[pl.ds(b * BLOCK, BLOCK), pl.ds(column, HD)] = out[g * BLOCK : (g + 1) * BLOCK]

    def head_columns(h):
        return pl.multiple_of(h * PER_HEAD, HD), pl.multiple_of(h * PER_HEAD + HD, HD)

    def fine(h, start, size, present):
        key_column, value_column = head_columns(h)
        k = kv0[pl.ds(start, size), pl.ds(key_column, HD)]
        v = kv0[pl.ds(start, size), pl.ds(value_column, HD)]
        if present is None:
            count = jnp.ones((size, HD), BF16)
        else:
            row = lax.broadcasted_iota(jnp.int32, (size, HD), 0)
            count = (row < jnp.where(present, size, 0)).astype(F32).astype(BF16)
        return k, jnp.concatenate([v, count], axis=1)

    def own_rows(h):
        for b in range(blocks):
            low, high = max(b, 1), min(b + 2, blocks)
            scored(h, b, *fine(h, low * BLOCK, (high - low + 1) * BLOCK, None), True, False)

    def swap_start(c):
        half_wait(c).wait_recv()
        swap_copy(c).start()
        pl.when(cross_up)(lambda: cross_copy(True, c).start())
        pl.when(cross_down)(lambda: cross_copy(False, c).start())

    def pass_start(c):
        swap_wait(c).wait_recv()
        pl.when(phase == 0)(lambda: pass_copy(True, c).start())
        pl.when(phase == 3)(lambda: pass_copy(False, c).start())

    def advance(step, c):
        step_wait(step, c).wait_recv()
        step_copy(step + 1, c).start()

    chunks = range(CHUNKS)
    last_step = len(bits) - 1 if spread else 0

    if not spread:
        over_window(direct_copy)

    for h in range(KVHEADS):
        if spread and 0 < h <= last_step - 2:
            for c in chunks:
                advance(h - 1, c)
        if h == 2:
            for c in chunks:
                swap_start(c)
        if h == KVHEADS - 1:
            if spread:
                for step in range(KVHEADS - 2, last_step - 1):
                    for c in chunks:
                        advance(step, c)
            halo_start(1, 0)
        own_rows(h)

    def arrived(c):
        pass_start(c)
        halo_start(0, c)
        if c + 1 < CHUNKS:
            halo_start(1, c + 1)
        if spread:
            advance(last_step - 1, c)

    def finish(c):
        columns = columns_of(c)
        if spread:
            step_wait(last_step, c).wait_recv()
        elif c == 0:
            over_window(lambda j, t: direct_wait(j, t).wait_recv())
        second = kv2[:, :, :, columns].astype(F32).reshape(level2, CHUNK).astype(BF16)
        kvc[pl.ds(level1, level2), columns] = second
        if spread:
            kvc[pl.ds(top_at, top_rows), columns] = pool_rows(second)
        elif c == 0:
            loads[-1].wait()
        pl.when(has_third)(lambda: third_wait(c).wait_recv())

    coarse_rows = level1 + level2 + top_rows
    row = lax.broadcasted_iota(jnp.int32, (coarse_rows, HD), 0)
    missing = ((row < jnp.where(a == 0, pair, 0))) | (
        (row >= jnp.where(a == last_pair, 2 * pair, level1)) & (row < level1)
    )
    if n > 2 * span2:
        missing = missing | (
            (row >= level1) & (row < top_at)
            & ((row < level1 + (low2 - base2) * rows2) | (row >= level1 + (high2 - base2) * rows2))
        )
    coarse_count = jnp.where(missing, 0.0, 1.0).astype(BF16)

    def coarse(h):
        key_column, value_column = head_columns(h)
        k = kvc[:, pl.ds(key_column, HD)]
        v = jnp.concatenate([kvc[:, pl.ds(value_column, HD)], coarse_count], axis=1)
        for b in range(blocks):
            scored(h, b, k, v, False, 0 < b < blocks - 1)

    def ends(h):
        scored(h, 0, *fine(h, 0, BLOCK, me > 0), False, blocks > 1)
        scored(h, blocks - 1, *fine(h, BLOCK + tok, BLOCK, me < n - 1), False, True)

    heads = KVHEADS // CHUNKS
    arrived(0)
    for c in chunks:
        finish(c)

        @pl.loop(c * heads, (c + 1) * heads - 1)
        def _(h):
            coarse(h)

        if c + 1 < CHUNKS:
            arrived(c + 1)
        coarse((c + 1) * heads - 1)

    for c in chunks:
        pl.when(me > 0)(lambda: halo_copy(True, c).wait_recv())
        pl.when(me + 1 < n)(lambda: halo_copy(False, c).wait_recv())

        @pl.loop(c * heads, (c + 1) * heads)
        def _(h):
            ends(h)

    for c in chunks:
        pl.when(me + 1 < n)(lambda: halo_copy(True, c).wait_send())
        pl.when(me > 0)(lambda: halo_copy(False, c).wait_send())
        half_copy(c).wait_send()
        swap_copy(c).wait_send()
        pl.when(cross_up)(lambda: cross_copy(True, c).wait_send())
        pl.when(cross_down)(lambda: cross_copy(False, c).wait_send())
        pl.when(phase == 0)(lambda: pass_copy(True, c).wait_send())
        pl.when(phase == 3)(lambda: pass_copy(False, c).wait_send())
    if spread:
        for step in range(len(bits)):
            for c in chunks:
                step_copy(step, c).wait_send()
    else:
        over_window(lambda j, t: direct_wait(j, t).wait_send())


def pool_level(rows):
    summed = rows.astype(F32).reshape(rows.shape[0] // POOL, POOL, rows.shape[1]).sum(axis=1)
    return (summed * POOL ** (-0.5)).astype(BF16)


def local(n_seq, n_outer, queries, keys, values):
    tok = queries.shape[0]
    n = n_seq * n_outer
    rows1, rows2 = tok // POOL, tok // POOL**2
    assert 2 * rows1 == BLOCK and n % 8 == 0
    held2 = min(3 * (BLOCK // rows2), n)
    spread = held2 == n and n & (n - 1) == 0
    operands = [queries, keys, values]
    if not spread:
        heads = [x.reshape(tok, KVHEADS, HD) for x in (keys, values)]
        joined = jnp.stack(heads, axis=2).reshape(tok, 2 * WIDTH)
        own = pool_level(pool_level(pool_level(joined)))
        operands.append(lax.all_gather(own, ("outer", "seq"), axis=0, tiled=True))
    coarse_rows = 3 * BLOCK + held2 * rows2 + n * tok // POOL**3
    units = KVHEADS * (tok // BLOCK)
    return pl.pallas_call(
        functools.partial(fused, n_seq, n_outer, spread),
        out_shape=jax.ShapeDtypeStruct((tok, QHEADS * HD), BF16),
        in_specs=[pl.BlockSpec(memory_space=pltpu.HBM)] * len(operands),
        out_specs=pl.BlockSpec(memory_space=pltpu.VMEM),
        scratch_shapes=[
            pltpu.VMEM((tok, QHEADS * HD), BF16),
            pltpu.VMEM((tok + 2 * BLOCK, 2 * WIDTH), BF16),
            pltpu.VMEM((coarse_rows, 2 * WIDTH), BF16),
            pltpu.VMEM((held2 // POOL, POOL, rows2, 2 * WIDTH), BF16),
            pltpu.VMEM((units, GROUP * BLOCK, HD), F32),
            pltpu.VMEM((units, GROUP * BLOCK, 2 * HD), F32),
            pltpu.SemaphoreType.DMA((2 * KVHEADS + 2,)),
            pltpu.SemaphoreType.DMA((CHUNKS, 2)),
            pltpu.SemaphoreType.DMA((CHUNKS, 2)),
            pltpu.SemaphoreType.DMA((CHUNKS, 4)),
            pltpu.SemaphoreType.DMA((CHUNKS, 3)),
            pltpu.SemaphoreType.DMA((CHUNKS, held2)),
            pltpu.SemaphoreType.DMA((CHUNKS, held2)),
        ],
        compiler_params=pltpu.CompilerParams(
            collective_id=0, has_side_effects=True, vmem_limit_bytes=58 * 1024 * 1024
        ),
    )(*operands)


def solution(mesh):
    spec = P(("outer", "seq"), None)
    return jax.shard_map(
        functools.partial(local, mesh.shape["seq"], mesh.shape["outer"]),
        mesh=mesh,
        in_specs=(spec, spec, spec),
        out_specs=spec,
        check_vma=False,
    )
```
